32 devices in a mesh: cell: 4 (over z), spot: 8 (over y, x, core).
Axes of the slice: x: 2, y: 2, z: 4, core: 2. Of those that a mesh axis runs over, the one named last changes fastest.
Arguments:
- logits: float32 [4096, 4096], P('cell', 'spot'), may hold values from -4 to 330
- first_moment: bfloat16 [4096, 4096], P('cell', 'spot'), may hold values from -3 to 3
- second_moment: bfloat16 [4096, 4096], P('cell', 'spot'), may hold values from 0.049804688 to 1
- cell_expr: bfloat16 [4096, 128], P('cell'), may hold values from -36 to 36
- spot_expr: float32 [4096, 128], P('spot'), may hold values from -500 to 500
Outputs:
- new_logits: float32 [4096, 4096], P('cell', 'spot')
- new_first_moment: bfloat16 [4096, 4096], P('cell', 'spot')
- new_second_moment: bfloat16 [4096, 4096], P('cell', 'spot')
The draws below stay inside these ranges and needn't reach their ends.
All inputs are finite; a program needn't handle non-finite values.
Results may differ from the reference program's by a relative error of at most 0.0052.
Values may be sent and summed in bfloat16 or wider, within the bound.
A program may use at most 64 MiB of HBM per device.

```python
import math
import jax
import jax.numpy as jnp
from jax import lax

GENES = 128
CELL_DEV = 1024
CELLS = 4096
SPOTS = 4096


def draw_logits(key, part):
    keys = jax.random.split(jax.random.fold_in(key, 11), 1)
    column = jnp.arange(SPOTS, dtype=jnp.float32)[None, :] / SPOTS
    base = jnp.clip(jax.random.normal(keys[0], (CELLS, SPOTS), jnp.float32), -4.0, 4.0)
    values = base + math.log(4.0) * column
    return values.astype(jnp.float32)


def draw_cell_expr(key, part):
    keys = jax.random.split(jax.random.fold_in(key, 23), 3)
    row_scale = 0.3 * jnp.exp(math.log(10.0) * jax.random.uniform(keys[0], (CELLS, 1), jnp.float32))
    gene_scale = 0.3 * jnp.exp(math.log(10.0) * jax.random.uniform(keys[1], (1, GENES), jnp.float32))
    noise = jnp.clip(jax.random.normal(keys[2], (CELLS, GENES), jnp.float32), -4.0, 4.0)
    values = noise * row_scale * gene_scale
    return values.astype(jnp.bfloat16)


def draw_spot_expr(key, part):
    keys = jax.random.split(jax.random.fold_in(key, 37), 3)
    position = jnp.arange(SPOTS, dtype=jnp.float32)[:, None] / SPOTS
    spot_scale = 0.3 * jnp.exp(math.log(10.0) * jax.random.uniform(keys[0], (SPOTS, 1), jnp.float32))
    gene_scale = 0.3 * jnp.exp(math.log(10.0) * jax.random.uniform(keys[1], (1, GENES), jnp.float32))
    noise = jnp.clip(jax.random.normal(keys[2], (SPOTS, GENES), jnp.float32), -4.0, 4.0)
    values = noise * spot_scale * gene_scale * jnp.exp(math.log(3.0) * position)
    return values.astype(jnp.float32)


def level_of(stream_key, extent, shards, least, high):
    def one(axis_at, shards_of):
        draws = jax.random.uniform(jax.random.fold_in(jax.random.fold_in(stream_key, 6), axis_at), (shards_of,), jnp.float32, least / len(shards), high / len(shards))
        return jnp.repeat(jnp.exp(draws), extent[axis_at] // shards_of).reshape((-1,) + (1,) * (len(extent) - axis_at - 1))

    loudness = one(*shards[0])
    for cut in shards[1:]:
        loudness = loudness * one(*cut)
    return loudness


def normal_values(rng, shape, width, limit, pieces=(), kind=jnp.bfloat16):
    array = width * jax.random.normal(rng, shape, jnp.float32)
    if pieces:
        array = array * level_of(rng, shape, pieces, -0.22, 0.18)
    return jnp.clip(array, -limit, limit).astype(kind)


def setup_inputs(seed: int = 0) -> dict:
    key_list = jax.random.split(jax.random.key(seed), 6)
    return {
        "logits": draw_logits(jax.random.fold_in(key_list[5], 71), 0),
        "first_moment": normal_values(key_list[1], (CELLS, SPOTS), 0.5, 3.0, ((0, 4), (1, 8))),
        "second_moment": jnp.clip(jnp.exp(math.log(1.0) - 2.9996462 * jax.random.uniform(key_list[2], (CELLS, SPOTS), jnp.float32) ** level_of(key_list[2], (CELLS, SPOTS), ((0, 4), (1, 8)), -0.2, 0.2)), 0.049804688, 1.0).astype(jnp.bfloat16),
        "cell_expr": draw_cell_expr(jax.random.fold_in(key_list[5], 71), 0),
        "spot_expr": draw_spot_expr(jax.random.fold_in(key_list[5], 71), 0),
    }


beta_one = 0.9
beta_two = 0.99
learn_rate = 0.1
adam_epsilon = 1e-08
norm_epsilon = 1e-06
adam_count = 10

def softmax_rows(block_logits):
    row_max = lax.optimization_barrier(jnp.max(block_logits, axis=1, keepdims=True))
    expo = jnp.exp(block_logits - row_max)
    return expo / lax.optimization_barrier(jnp.sum(expo, axis=1, keepdims=True))

def reference(logits, first_moment, second_moment, cell_expr, spot_expr):
    blocks = CELLS // CELL_DEV
    logit_blocks = logits.reshape(blocks, CELL_DEV, SPOTS)
    expr_blocks = cell_expr.reshape(blocks, CELL_DEV, GENES)
    first_blocks = first_moment.reshape(blocks, CELL_DEV, SPOTS)
    second_blocks = second_moment.reshape(blocks, CELL_DEV, SPOTS)

    def accumulate(running, inputs):
        block_logits, block_expr = inputs
        weights = softmax_rows(block_logits).astype(jnp.bfloat16)
        return (running + jnp.dot(weights.T, block_expr, preferred_element_type=jnp.float32), None)
    predicted, unused = lax.scan(accumulate, jnp.zeros((SPOTS, GENES), jnp.float32), (logit_blocks, expr_blocks))
    spot_dot = lax.optimization_barrier(jnp.sum(predicted * spot_expr, axis=1, keepdims=True))
    spot_pred = lax.optimization_barrier(jnp.sum(predicted * predicted, axis=1, keepdims=True))
    spot_target = lax.optimization_barrier(jnp.sum(spot_expr * spot_expr, axis=1, keepdims=True))
    gene_dot = lax.optimization_barrier(jnp.sum(predicted * spot_expr, axis=0, keepdims=True))
    gene_pred = lax.optimization_barrier(jnp.sum(predicted * predicted, axis=0, keepdims=True))
    gene_target = lax.optimization_barrier(jnp.sum(spot_expr * spot_expr, axis=0, keepdims=True))
    loss_weight = jnp.sqrt(jnp.float32(GENES * CELLS))
    by_spot = (spot_expr - spot_dot / (spot_pred + norm_epsilon) * predicted) / jnp.sqrt((spot_pred + norm_epsilon) * (spot_target + norm_epsilon))
    by_gene = (spot_expr - gene_dot / (gene_pred + norm_epsilon) * predicted) / jnp.sqrt((gene_pred + norm_epsilon) * (gene_target + norm_epsilon))
    pred_grad = -loss_weight * (by_spot + SPOTS / GENES * by_gene)
    grad_rounded = pred_grad.astype(jnp.bfloat16)

    def update(inputs):
        block_logits, block_first, block_second, block_expr = inputs
        probs = softmax_rows(block_logits)
        prob_grad = jnp.dot(block_expr, grad_rounded.T, preferred_element_type=jnp.float32)
        row_dot = lax.optimization_barrier(jnp.sum(probs * prob_grad, axis=1, keepdims=True))
        logit_grad = probs * (prob_grad - row_dot)
        first_new = beta_one * block_first.astype(jnp.float32) + (1.0 - beta_one) * logit_grad
        second_new = beta_two * block_second.astype(jnp.float32) + (1.0 - beta_two) * logit_grad * logit_grad
        first_hat = first_new / (1.0 - beta_one ** adam_count)
        second_hat = second_new / (1.0 - beta_two ** adam_count)
        stepped = block_logits - learn_rate * first_hat / (jnp.sqrt(second_hat) + adam_epsilon)
        return (stepped, first_new.astype(jnp.bfloat16), second_new.astype(jnp.bfloat16))
    stepped, first_out, second_out = lax.map(update, (logit_blocks, first_blocks, second_blocks, expr_blocks))
    return (stepped.reshape(CELLS, SPOTS), first_out.reshape(CELLS, SPOTS), second_out.reshape(CELLS, SPOTS))
```

```python
import functools

import jax
import jax.numpy as jnp
from jax import lax
from jax.experimental import pallas as pl
from jax.experimental.pallas import tpu as pltpu
from jax.sharding import PartitionSpec as P

beta_one = 0.9
beta_two = 0.99
learn_rate = 0.1
adam_epsilon = 1e-08
norm_epsilon = 1e-06
adam_count = 10

MESH = pl.DeviceIdType.MESH
LANES = 128
WIRE = jnp.float32


def eye_mask():
    row = lax.broadcasted_iota(jnp.int32, (LANES, LANES), 0)
    lane = lax.broadcasted_iota(jnp.int32, (LANES, LANES), 1)
    return row == lane


def to_row(column, mask):
    wide = jnp.broadcast_to(column, (column.shape[0], LANES))
    return jnp.sum(jnp.where(mask[: column.shape[0]], wide, 0.0), axis=0, keepdims=True)


def to_column(row, mask, count=LANES):
    wide = jnp.broadcast_to(row, (count, LANES))
    return jnp.sum(jnp.where(mask[:count], wide, 0.0), axis=1, keepdims=True)


def exchange_kernel(
    cell_n, spot_n, cells, spots,
    logits_hbm, expr_hbm, target_hbm,
    stats_out, grad_out,
    logits, expr, target, probs, weights, expr_t, target_t, part,
    stat_mine, stat_peer, part_peer, spot_mine, spot_peer, gene_mine, gene_peer,
    grads, dots_mine, dots_peer,
    load_sem, stat_send, stat_recv, part_send, part_recv, sums_send, sums_recv,
    gene_send, gene_recv, grad_send, grad_recv, dots_send, dots_recv,
):
    rows, width = logits.shape
    genes = expr.shape[1]
    own_genes = genes // cell_n
    chunks = rows // LANES
    loss_weight = float(genes * cells) ** 0.5
    ratio = spots / genes
    my_cell = lax.axis_index("cell")
    my_spot = lax.axis_index("spot")

    def cell_peer(k):
        return (lax.rem(my_cell + k, cell_n), my_spot)

    def spot_peer_id(k):
        return (my_cell, lax.rem(my_spot + k, spot_n))

    loads = [
        pltpu.make_async_copy(
            logits_hbm.at[pl.ds(i * LANES, LANES)], logits.at[pl.ds(i * LANES, LANES)], load_sem.at[i]
        )
        for i in range(chunks)
    ]
    loads.append(pltpu.make_async_copy(expr_hbm, expr, load_sem.at[chunks]))
    loads.append(pltpu.make_async_copy(target_hbm, target, load_sem.at[chunks + 1]))
    for load in loads:
        load.start()
    barrier = pltpu.get_barrier_semaphore()
    for k in range(1, cell_n):
        pl.semaphore_signal(barrier, inc=1, device_id=cell_peer(k), device_id_type=MESH)
    for k in range(1, spot_n):
        pl.semaphore_signal(barrier, inc=1, device_id=spot_peer_id(k), device_id_type=MESH)

    mask = eye_mask()

    for i in range(chunks):
        loads[i].wait()
        block = logits[i * LANES : (i + 1) * LANES, :]
        top = jnp.max(block, axis=1, keepdims=True)
        expo = jnp.exp(block - top)
        probs[i * LANES : (i + 1) * LANES, :] = expo
        stat_mine[i : i + 1, :] = to_row(top, mask)
        stat_mine[chunks + i : chunks + i + 1, :] = to_row(
            jnp.sum(expo, axis=1, keepdims=True), mask
        )

    pl.semaphore_wait(barrier, cell_n + spot_n - 2)

    def send(src, dst, send_sem, recv_sem, device):
        copy = pltpu.make_async_remote_copy(
            src_ref=src, dst_ref=dst, send_sem=send_sem, recv_sem=recv_sem,
            device_id=device, device_id_type=MESH,
        )
        copy.start()
        return copy

    stat_copies = [
        send(stat_mine, stat_peer.at[k - 1], stat_send.at[k - 1], stat_recv.at[k - 1], spot_peer_id(k))
        for k in range(1, spot_n)
    ]
    loads[chunks].wait()
    loads[chunks + 1].wait()
    expr_t[...] = expr[...].astype(jnp.float32).T.astype(jnp.bfloat16)
    flipped = target[...].T
    target_t[...] = flipped.reshape(target_t.shape)
    spot_target = jnp.sum(flipped * flipped, axis=0, keepdims=True)
    own_target = target_t[my_cell]
    gene_mine[2:3, :] = to_row(jnp.sum(own_target * own_target, axis=1, keepdims=True), mask)
    for copy in stat_copies:
        copy.wait()

    local_max = stat_mine[:chunks, :]
    row_max = local_max
    for k in range(spot_n - 1):
        row_max = jnp.maximum(row_max, stat_peer[k, :chunks, :])
    row_total = stat_mine[chunks:, :] * jnp.exp(local_max - row_max)
    for k in range(spot_n - 1):
        row_total = row_total + stat_peer[k, chunks:, :] * jnp.exp(stat_peer[k, :chunks, :] - row_max)
    factor = jnp.exp(local_max - row_max) / row_total
    stats_out[:chunks, :] = row_max
    stats_out[chunks : 2 * chunks, :] = 1.0 / row_total
    for i in range(chunks):
        part_rows = slice(i * LANES, (i + 1) * LANES)
        prob = probs[part_rows, :] * to_column(factor[i : i + 1, :], mask)
        probs[part_rows, :] = prob
        weights[part_rows, :] = prob.astype(jnp.bfloat16)
    partial = jnp.dot(expr_t[...], weights[...], preferred_element_type=jnp.float32)
    part[...] = partial.astype(part.dtype).reshape(part.shape)

    part_copies = [
        send(part.at[lax.rem(my_cell + k, cell_n)], part_peer.at[k - 1], part_send.at[k - 1],
             part_recv.at[k - 1], cell_peer(k))
        for k in range(1, cell_n)
    ]
    for copy in part_copies:
        copy.wait()
    predicted = part[my_cell].astype(jnp.float32)
    for k in range(cell_n - 1):
        predicted = predicted + part_peer[k].astype(jnp.float32)

    product = predicted * own_target
    square = predicted * predicted
    spot_mine[0:1, :] = jnp.sum(product, axis=0, keepdims=True)
    spot_mine[1:2, :] = jnp.sum(square, axis=0, keepdims=True)
    spot_copies = [
        send(spot_mine, spot_peer.at[k - 1], sums_send.at[k - 1], sums_recv.at[k - 1], cell_peer(k))
        for k in range(1, cell_n)
    ]
    gene_mine[0:1, :] = to_row(jnp.sum(product, axis=1, keepdims=True), mask)
    gene_mine[1:2, :] = to_row(jnp.sum(square, axis=1, keepdims=True), mask)
    gene_copies = [
        send(gene_mine, gene_peer.at[k - 1], gene_send.at[k - 1], gene_recv.at[k - 1], spot_peer_id(k))
        for k in range(1, spot_n)
    ]
    for copy in gene_copies:
        copy.wait()
    gene_sums = gene_mine[...]
    for k in range(spot_n - 1):
        gene_sums = gene_sums + gene_peer[k]
    gene_scale = lax.rsqrt((gene_sums[1:2] + norm_epsilon) * (gene_sums[2:3] + norm_epsilon))
    gene_lean = gene_sums[0:1] / (gene_sums[1:2] + norm_epsilon)
    gene_scale = to_column(gene_scale, mask, own_genes)
    gene_lean = to_column(gene_lean, mask, own_genes)
    by_gene = (own_target - gene_lean * predicted) * gene_scale
    for copy in spot_copies:
        copy.wait()
    spot_sums = spot_mine[...]
    for k in range(cell_n - 1):
        spot_sums = spot_sums + spot_peer[k]
    spot_scale = lax.rsqrt((spot_sums[1:2] + norm_epsilon) * (spot_target + norm_epsilon))
    spot_lean = spot_sums[0:1] / (spot_sums[1:2] + norm_epsilon)
    by_spot = (own_target - spot_lean * predicted) * spot_scale
    grad = -loss_weight * (by_spot + ratio * by_gene)
    grads[my_cell] = grad.astype(jnp.bfloat16)
    grad_copies = [
        send(grads.at[my_cell], grads.at[my_cell], grad_send.at[k - 1], grad_recv.at[k - 1], cell_peer(k))
        for k in range(1, cell_n)
    ]
    for copy in grad_copies:
        copy.wait()
    grad_all = grads[...].reshape(genes, width)
    grad_out[...] = grad_all
    for i in range(chunks):
        part_rows = slice(i * LANES, (i + 1) * LANES)
        prob_grad = jnp.dot(expr[part_rows, :], grad_all, preferred_element_type=jnp.float32)
        dots_mine[i : i + 1, :] = to_row(
            jnp.sum(probs[part_rows, :] * prob_grad, axis=1, keepdims=True), mask
        )
    dots_copies = [
        send(dots_mine, dots_peer.at[k - 1], dots_send.at[k - 1], dots_recv.at[k - 1], spot_peer_id(k))
        for k in range(1, spot_n)
    ]
    for copy in dots_copies:
        copy.wait()
    row_dot = dots_mine[...]
    for k in range(spot_n - 1):
        row_dot = row_dot + dots_peer[k]
    stats_out[2 * chunks :, :] = row_dot


def update_kernel(
    chunks, stats, grad, logits, first, second, expr, new_logits, new_first, new_second
):
    at = pl.program_id(0)
    mask = eye_mask()
    per = logits.shape[0] // LANES
    for j in range(per):
        span = slice(j * LANES, (j + 1) * LANES)
        row = at * per + j
        row_max = to_column(stats[pl.ds(row, 1), :], mask)
        scale = to_column(stats[pl.ds(chunks + row, 1), :], mask)
        row_dot = to_column(stats[pl.ds(2 * chunks + row, 1), :], mask)
        block = logits[span, :]
        prob = jnp.exp(block - row_max) * scale
        prob_grad = jnp.dot(expr[span, :], grad[...], preferred_element_type=jnp.float32)
        logit_grad = prob * (prob_grad - row_dot)
        first_new = beta_one * first[span, :].astype(jnp.float32) + (1.0 - beta_one) * logit_grad
        second_new = (
            beta_two * second[span, :].astype(jnp.float32)
            + (1.0 - beta_two) * logit_grad * logit_grad
        )
        first_hat = first_new * (learn_rate / (1.0 - beta_one**adam_count))
        second_hat = second_new * (1.0 / (1.0 - beta_two**adam_count))
        new_logits[span, :] = block - first_hat / (jnp.sqrt(second_hat) + adam_epsilon)
        new_first[span, :] = first_new.astype(jnp.bfloat16)
        new_second[span, :] = second_new.astype(jnp.bfloat16)


def body(cell_n, spot_n, logits, first_moment, second_moment, cell_expr, spot_expr):
    rows, width = logits.shape
    genes = cell_expr.shape[1]
    own_genes = genes // cell_n
    chunks = rows // LANES
    f32 = jnp.float32
    dma = pltpu.SemaphoreType.DMA
    anywhere = pl.BlockSpec(memory_space=pl.ANY)
    in_vmem = pl.BlockSpec(memory_space=pltpu.VMEM)
    cell_sem = dma((cell_n - 1,))
    spot_sem = dma((spot_n - 1,))
    stats, grad = pl.pallas_call(
        functools.partial(exchange_kernel, cell_n, spot_n, rows * cell_n, width * spot_n),
        out_shape=(
            jax.ShapeDtypeStruct((3 * chunks, LANES), f32),
            jax.ShapeDtypeStruct((genes, width), jnp.bfloat16),
        ),
        in_specs=[anywhere] * 3,
        out_specs=(in_vmem, in_vmem),
        scratch_shapes=[
            pltpu.VMEM((rows, width), f32),
            pltpu.VMEM((rows, genes), jnp.bfloat16),
            pltpu.VMEM((width, genes), f32),
            pltpu.VMEM((rows, width), f32),
            pltpu.VMEM((rows, width), jnp.bfloat16),
            pltpu.VMEM((genes, rows), jnp.bfloat16),
            pltpu.VMEM((cell_n, own_genes, width), f32),
            pltpu.VMEM((cell_n, own_genes, width), WIRE),
            pltpu.VMEM((2 * chunks, LANES), f32),
            pltpu.VMEM((spot_n - 1, 2 * chunks, LANES), f32),
            pltpu.VMEM((cell_n - 1, own_genes, width), WIRE),
            pltpu.VMEM((2, width), f32),
            pltpu.VMEM((cell_n - 1, 2, width), f32),
            pltpu.VMEM((3, LANES), f32),
            pltpu.VMEM((spot_n - 1, 3, LANES), f32),
            pltpu.VMEM((cell_n, own_genes, width), jnp.bfloat16),
            pltpu.VMEM((chunks, LANES), f32),
            pltpu.VMEM((spot_n - 1, chunks, LANES), f32),
            dma((chunks + 2,)),
            spot_sem, spot_sem, cell_sem, cell_sem, cell_sem, cell_sem,
            spot_sem, spot_sem, cell_sem, cell_sem, spot_sem, spot_sem,
        ],
        compiler_params=pltpu.CompilerParams(
            collective_id=0, has_side_effects=True, vmem_limit_bytes=32 << 20
        ),
        name="exchange",
    )(logits, cell_expr, spot_expr)
    tile = 2 * LANES if rows % (2 * LANES) == 0 else LANES
    by_row = pl.BlockSpec((tile, width), lambda i: (i, 0))
    return pl.pallas_call(
        functools.partial(update_kernel, chunks),
        grid=(rows // tile,),
        out_shape=(
            jax.ShapeDtypeStruct(logits.shape, f32),
            jax.ShapeDtypeStruct(logits.shape, jnp.bfloat16),
            jax.ShapeDtypeStruct(logits.shape, jnp.bfloat16),
        ),
        in_specs=[
            pl.BlockSpec(stats.shape, lambda i: (0, 0)),
            pl.BlockSpec(grad.shape, lambda i: (0, 0)),
            by_row,
            by_row,
            by_row,
            pl.BlockSpec((tile, genes), lambda i: (i, 0)),
        ],
        out_specs=(by_row, by_row, by_row),
        name="update",
    )(stats, grad, logits, first_moment, second_moment, cell_expr)


def solution(mesh):
    placed = (
        P("cell", "spot"),
        P("cell", "spot"),
        P("cell", "spot"),
        P("cell", None),
        P("spot", None),
    )
    return jax.shard_map(
        functools.partial(body, mesh.shape["cell"], mesh.shape["spot"]),
        mesh=mesh,
        in_specs=placed,
        out_specs=(P("cell", "spot"), P("cell", "spot"), P("cell", "spot")),
        check_vma=False,
    )
```

```python
import functools

import jax
import jax.numpy as jnp
from jax import lax
from jax.experimental import pallas as pl
from jax.experimental.pallas import tpu as pltpu
from jax.sharding import PartitionSpec as P

beta_one = 0.9
beta_two = 0.99
learn_rate = 0.1
adam_epsilon = 1e-08
norm_epsilon = 1e-06
adam_count = 10

MESH = pl.DeviceIdType.MESH
LANES = 128
WIRE = jnp.bfloat16


def eye_mask():
    row = lax.broadcasted_iota(jnp.int32, (LANES, LANES), 0)
    lane = lax.broadcasted_iota(jnp.int32, (LANES, LANES), 1)
    return row == lane


def to_row(column, mask):
    wide = jnp.broadcast_to(column, (column.shape[0], LANES))
    return jnp.sum(jnp.where(mask[: column.shape[0]], wide, 0.0), axis=0, keepdims=True)


def to_column(row, mask, count=LANES):
    wide = jnp.broadcast_to(row, (count, LANES))
    return jnp.sum(jnp.where(mask[:count], wide, 0.0), axis=1, keepdims=True)


def exchange_kernel(
    cell_n, spot_n, cells, spots,
    logits_hbm, expr_hbm, target_hbm, first_hbm, second_hbm,
    logits, first, second, probs, prob_grads, row_dots,
    expr, target, weights, expr_t, target_t, own_part, part,
    stat_mine, stat_peer, part_peer, spot_mine, spot_peer, gene_mine, gene_peer,
    grads, dots_mine, dots_peer,
    load_sem, stat_send, stat_recv, part_send, part_recv, sums_send, sums_recv,
    gene_send, gene_recv, grad_send, grad_recv, dots_send, dots_recv,
):
    rows, width = logits.shape
    genes = expr.shape[1]
    own_genes = genes // cell_n
    chunks = rows // LANES
    loss_weight = float(genes * cells) ** 0.5
    ratio = spots / genes
    my_cell = lax.axis_index("cell")
    my_spot = lax.axis_index("spot")

    def cell_peer(k):
        return (lax.rem(my_cell + k, cell_n), my_spot)

    def spot_peer_id(k):
        return (my_cell, lax.rem(my_spot + k, spot_n))

    loads = [
        pltpu.make_async_copy(
            logits_hbm.at[pl.ds(i * LANES, LANES)], logits.at[pl.ds(i * LANES, LANES)], load_sem.at[i]
        )
        for i in range(chunks)
    ]
    loads.append(pltpu.make_async_copy(expr_hbm, expr, load_sem.at[chunks]))
    loads.append(pltpu.make_async_copy(target_hbm, target, load_sem.at[chunks + 1]))
    loads.append(pltpu.make_async_copy(first_hbm, first, load_sem.at[chunks + 2]))
    loads.append(pltpu.make_async_copy(second_hbm, second, load_sem.at[chunks + 3]))
    for load in loads:
        load.start()
    barrier = pltpu.get_barrier_semaphore()
    for k in range(1, cell_n):
        pl.semaphore_signal(barrier, inc=1, device_id=cell_peer(k), device_id_type=MESH)
    for k in range(1, spot_n):
        pl.semaphore_signal(barrier, inc=1, device_id=spot_peer_id(k), device_id_type=MESH)

    mask = eye_mask()

    for i in range(chunks):
        loads[i].wait()
        block = logits[i * LANES : (i + 1) * LANES, :]
        top = jnp.max(block, axis=1, keepdims=True)
        expo = jnp.exp(block - top)
        probs[i * LANES : (i + 1) * LANES, :] = expo
        stat_mine[i : i + 1, :] = to_row(top, mask)
        stat_mine[chunks + i : chunks + i + 1, :] = to_row(
            jnp.sum(expo, axis=1, keepdims=True), mask
        )

    pl.semaphore_wait(barrier, cell_n + spot_n - 2)

    def send(src, dst, send_sem, recv_sem, device):
        copy = pltpu.make_async_remote_copy(
            src_ref=src, dst_ref=dst, send_sem=send_sem, recv_sem=recv_sem,
            device_id=device, device_id_type=MESH,
        )
        copy.start()
        return copy

    stat_copies = [
        send(stat_mine, stat_peer.at[k - 1], stat_send.at[k - 1], stat_recv.at[k - 1], spot_peer_id(k))
        for k in range(1, spot_n)
    ]
    loads[chunks].wait()
    loads[chunks + 1].wait()
    expr_t[...] = expr[...].astype(jnp.float32).T.astype(jnp.bfloat16)
    flipped = target[...].T
    target_t[...] = flipped.reshape(target_t.shape)
    spot_target = jnp.sum(flipped * flipped, axis=0, keepdims=True)
    own_target = target_t[my_cell]
    gene_mine[2:3, :] = to_row(jnp.sum(own_target * own_target, axis=1, keepdims=True), mask)
    for copy in stat_copies:
        copy.wait()

    local_max = stat_mine[:chunks, :]
    row_max = local_max
    for k in range(spot_n - 1):
        row_max = jnp.maximum(row_max, stat_peer[k, :chunks, :])
    row_total = stat_mine[chunks:, :] * jnp.exp(local_max - row_max)
    for k in range(spot_n - 1):
        row_total = row_total + stat_peer[k, chunks:, :] * jnp.exp(stat_peer[k, :chunks, :] - row_max)
    factor = jnp.exp(local_max - row_max) / row_total
    for i in range(chunks):
        part_rows = slice(i * LANES, (i + 1) * LANES)
        prob = probs[part_rows, :] * to_column(factor[i : i + 1, :], mask)
        probs[part_rows, :] = prob
        weights[part_rows, :] = prob.astype(jnp.bfloat16)
    partial = jnp.dot(expr_t[...], weights[...], preferred_element_type=jnp.float32)
    part[...] = partial.astype(part.dtype).reshape(part.shape)
    own_part[...] = partial.reshape(own_part.shape)

    part_copies = [
        send(part.at[lax.rem(my_cell + k, cell_n)], part_peer.at[k - 1], part_send.at[k - 1],
             part_recv.at[k - 1], cell_peer(k))
        for k in range(1, cell_n)
    ]
    for copy in part_copies:
        copy.wait()
    predicted = own_part[my_cell]
    for k in range(cell_n - 1):
        predicted = predicted + part_peer[k].astype(jnp.float32)

    product = predicted * own_target
    square = predicted * predicted
    spot_mine[0:1, :] = jnp.sum(product, axis=0, keepdims=True)
    spot_mine[1:2, :] = jnp.sum(square, axis=0, keepdims=True)
    spot_copies = [
        send(spot_mine, spot_peer.at[k - 1], sums_send.at[k - 1], sums_recv.at[k - 1], cell_peer(k))
        for k in range(1, cell_n)
    ]
    gene_mine[0:1, :] = to_row(jnp.sum(product, axis=1, keepdims=True), mask)
    gene_mine[1:2, :] = to_row(jnp.sum(square, axis=1, keepdims=True), mask)
    gene_copies = [
        send(gene_mine, gene_peer.at[k - 1], gene_send.at[k - 1], gene_recv.at[k - 1], spot_peer_id(k))
        for k in range(1, spot_n)
    ]
    for copy in gene_copies:
        copy.wait()
    gene_sums = gene_mine[...]
    for k in range(spot_n - 1):
        gene_sums = gene_sums + gene_peer[k]
    gene_scale = lax.rsqrt((gene_sums[1:2] + norm_epsilon) * (gene_sums[2:3] + norm_epsilon))
    gene_lean = gene_sums[0:1] / (gene_sums[1:2] + norm_epsilon)
    gene_scale = to_column(gene_scale, mask, own_genes)
    gene_lean = to_column(gene_lean, mask, own_genes)
    by_gene = (own_target - gene_lean * predicted) * gene_scale
    for copy in spot_copies:
        copy.wait()
    spot_sums = spot_mine[...]
    for k in range(cell_n - 1):
        spot_sums = spot_sums + spot_peer[k]
    spot_scale = lax.rsqrt((spot_sums[1:2] + norm_epsilon) * (spot_target + norm_epsilon))
    spot_lean = spot_sums[0:1] / (spot_sums[1:2] + norm_epsilon)
    by_spot = (own_target - spot_lean * predicted) * spot_scale
    grad = -loss_weight * (by_spot + ratio * by_gene)
    grads[my_cell] = grad.astype(jnp.bfloat16)
    grad_copies = [
        send(grads.at[my_cell], grads.at[my_cell], grad_send.at[k - 1], grad_recv.at[k - 1], cell_peer(k))
        for k in range(1, cell_n)
    ]
    for copy in grad_copies:
        copy.wait()
    grad_all = grads[...].reshape(genes, width)
    for i in range(chunks):
        part_rows = slice(i * LANES, (i + 1) * LANES)
        prob_grad = jnp.dot(expr[part_rows, :], grad_all, preferred_element_type=jnp.float32)
        prob_grads[part_rows, :] = prob_grad
        dots_mine[i : i + 1, :] = to_row(
            jnp.sum(probs[part_rows, :] * prob_grad, axis=1, keepdims=True), mask
        )
    dots_copies = [
        send(dots_mine, dots_peer.at[k - 1], dots_send.at[k - 1], dots_recv.at[k - 1], spot_peer_id(k))
        for k in range(1, spot_n)
    ]
    loads[chunks + 2].wait()
    loads[chunks + 3].wait()
    for copy in dots_copies:
        copy.wait()
    row_dot = dots_mine[...]
    for k in range(spot_n - 1):
        row_dot = row_dot + dots_peer[k]
    row_dots[...] = row_dot


def update_kernel(
    logits, first, second, probs, prob_grads, row_dots, new_logits, new_first, new_second
):
    at = pl.program_id(0)
    mask = eye_mask()
    per = new_logits.shape[0] // LANES
    for j in range(per):
        span = slice(j * LANES, (j + 1) * LANES)
        row = at * per + j
        rows = pl.ds(pl.multiple_of(row * LANES, LANES), LANES)
        row_dot = to_column(row_dots[pl.ds(row, 1), :], mask)
        logit_grad = probs[rows, :] * (prob_grads[rows, :] - row_dot)
        first_new = beta_one * first[rows, :].astype(jnp.float32) + (1.0 - beta_one) * logit_grad
        second_new = (
            beta_two * second[rows, :].astype(jnp.float32)
            + (1.0 - beta_two) * logit_grad * logit_grad
        )
        first_hat = first_new * (learn_rate / (1.0 - beta_one**adam_count))
        second_hat = second_new * (1.0 / (1.0 - beta_two**adam_count))
        new_logits[span, :] = logits[rows, :] - first_hat / (jnp.sqrt(second_hat) + adam_epsilon)
        new_first[span, :] = first_new.astype(jnp.bfloat16)
        new_second[span, :] = second_new.astype(jnp.bfloat16)


def body(cell_n, spot_n, logits, first_moment, second_moment, cell_expr, spot_expr):
    rows, width = logits.shape
    genes = cell_expr.shape[1]
    own_genes = genes // cell_n
    chunks = rows // LANES
    f32 = jnp.float32
    dma = pltpu.SemaphoreType.DMA
    in_hbm = pl.BlockSpec(memory_space=pltpu.HBM)
    in_vmem = pl.BlockSpec(memory_space=pltpu.VMEM)
    cell_sem = dma((cell_n - 1,))
    spot_sem = dma((spot_n - 1,))
    like = [jax.ShapeDtypeStruct(x.shape, x.dtype) for x in (logits, first_moment, second_moment)]
    operands = (logits, cell_expr, spot_expr, first_moment, second_moment)
    held = pl.pallas_call(
        functools.partial(exchange_kernel, cell_n, spot_n, rows * cell_n, width * spot_n),
        out_shape=(*like, like[0], like[0], jax.ShapeDtypeStruct((chunks, LANES), f32)),
        in_specs=[in_hbm] * 5,
        out_specs=(in_vmem,) * 6,
        scratch_shapes=[
            pltpu.VMEM((rows, genes), jnp.bfloat16),
            pltpu.VMEM((width, genes), f32),
            pltpu.VMEM((rows, width), jnp.bfloat16),
            pltpu.VMEM((genes, rows), jnp.bfloat16),
            pltpu.VMEM((cell_n, own_genes, width), f32),
            pltpu.VMEM((cell_n, own_genes, width), f32),
            pltpu.VMEM((cell_n, own_genes, width), WIRE),
            pltpu.VMEM((2 * chunks, LANES), f32),
            pltpu.VMEM((spot_n - 1, 2 * chunks, LANES), f32),
            pltpu.VMEM((cell_n - 1, own_genes, width), WIRE),
            pltpu.VMEM((2, width), f32),
            pltpu.VMEM((cell_n - 1, 2, width), f32),
            pltpu.VMEM((3, LANES), f32),
            pltpu.VMEM((spot_n - 1, 3, LANES), f32),
            pltpu.VMEM((cell_n, own_genes, width), jnp.bfloat16),
            pltpu.VMEM((chunks, LANES), f32),
            pltpu.VMEM((spot_n - 1, chunks, LANES), f32),
            dma((chunks + 4,)),
            spot_sem, spot_sem, cell_sem, cell_sem, cell_sem, cell_sem,
            spot_sem, spot_sem, cell_sem, cell_sem, spot_sem, spot_sem,
        ],
        compiler_params=pltpu.CompilerParams(
            collective_id=0, has_side_effects=True, vmem_limit_bytes=24 << 20
        ),
        cost_estimate=pl.CostEstimate(
            flops=4 * rows * width * genes, bytes_accessed=32 * rows * width, transcendentals=rows * width
        ),
        name="exchange",
    )(*(pltpu.with_memory_space_constraint(x, pltpu.HBM) for x in operands))
    tile = 2 * LANES if rows % (2 * LANES) == 0 else LANES
    by_row = pl.BlockSpec((tile, width), lambda i: (i, 0))
    return pl.pallas_call(
        update_kernel,
        grid=(rows // tile,),
        out_shape=like,
        in_specs=[in_vmem] * 6,
        out_specs=(by_row, by_row, by_row),
        compiler_params=pltpu.CompilerParams(vmem_limit_bytes=16 << 20),
        name="update",
    )(*held)


def solution(mesh):
    placed = (
        P("cell", "spot"),
        P("cell", "spot"),
        P("cell", "spot"),
        P("cell", None),
        P("spot", None),
    )
    return jax.shard_map(
        functools.partial(body, mesh.shape["cell"], mesh.shape["spot"]),
        mesh=mesh,
        in_specs=placed,
        out_specs=(P("cell", "spot"), P("cell", "spot"), P("cell", "spot")),
        check_vma=False,
    )
```

```python
import functools

import jax
import jax.numpy as jnp
from jax import lax
from jax.experimental import pallas as pl
from jax.experimental.pallas import tpu as pltpu
from jax.sharding import PartitionSpec as P

beta_one = 0.9
beta_two = 0.99
learn_rate = 0.1
adam_epsilon = 1e-08
norm_epsilon = 1e-06
adam_count = 10

MESH = pl.DeviceIdType.MESH
LANES = 128
WIRE = jnp.bfloat16


def eye_mask():
    row = lax.broadcasted_iota(jnp.int32, (LANES, LANES), 0)
    lane = lax.broadcasted_iota(jnp.int32, (LANES, LANES), 1)
    return row == lane


def to_row(column, mask):
    wide = jnp.broadcast_to(column, (column.shape[0], LANES))
    return jnp.sum(jnp.where(mask[: column.shape[0]], wide, 0.0), axis=0, keepdims=True)


def to_column(row, mask, count=LANES):
    wide = jnp.broadcast_to(row, (count, LANES))
    return jnp.sum(jnp.where(mask[:count], wide, 0.0), axis=1, keepdims=True)


def exchange_kernel(
    cell_n, spot_n, cells, spots,
    logits_hbm, expr_hbm, target_hbm, first_hbm, second_hbm,
    logits, first, second, probs, prob_grads, row_dots,
    expr, target, weights, expr_t, target_t, own_part, part,
    stat_mine, stat_peer, part_peer, gene_mine, gene_peer, shared, grads, dots_mine, dots_peer,
    load_sem, stat_send, stat_recv, part_send, part_recv,
    gene_send, gene_recv, shared_send, shared_recv, dots_send, dots_recv,
):
    rows, width = logits.shape
    genes = expr.shape[1]
    own_genes = genes // cell_n
    chunks = rows // LANES
    loss_weight = float(genes * cells) ** 0.5
    ratio = spots / genes
    my_cell = lax.axis_index("cell")
    my_spot = lax.axis_index("spot")

    def cell_peer(k):
        return (lax.rem(my_cell + k, cell_n), my_spot)

    def spot_peer_id(k):
        return (my_cell, lax.rem(my_spot + k, spot_n))

    loads = [
        pltpu.make_async_copy(
            logits_hbm.at[pl.ds(i * LANES, LANES)], logits.at[pl.ds(i * LANES, LANES)], load_sem.at[i]
        )
        for i in range(chunks)
    ]
    loads.append(pltpu.make_async_copy(expr_hbm, expr, load_sem.at[chunks]))
    loads.append(pltpu.make_async_copy(target_hbm, target, load_sem.at[chunks + 1]))
    loads.append(pltpu.make_async_copy(first_hbm, first, load_sem.at[chunks + 2]))
    loads.append(pltpu.make_async_copy(second_hbm, second, load_sem.at[chunks + 3]))
    for load in loads[: chunks + 2]:
        load.start()
    others = [(a, k) for k in range(spot_n) for a in range(cell_n) if a or k]

    def other(a, k):
        return (lax.rem(my_cell + a, cell_n), lax.rem(my_spot + k, spot_n))

    barrier = pltpu.get_barrier_semaphore()
    for a, k in others:
        pl.semaphore_signal(barrier, inc=1, device_id=other(a, k), device_id_type=MESH)

    mask = eye_mask()

    for i in range(chunks):
        loads[i].wait()
        block = logits[i * LANES : (i + 1) * LANES, :]
        top = jnp.max(block, axis=1, keepdims=True)
        expo = jnp.exp(block - top)
        probs[i * LANES : (i + 1) * LANES, :] = expo
        stat_mine[i : i + 1, :] = to_row(top, mask)
        stat_mine[chunks + i : chunks + i + 1, :] = to_row(
            jnp.sum(expo, axis=1, keepdims=True), mask
        )

    pl.semaphore_wait(barrier, len(others))

    def send(src, dst, send_sem, recv_sem, device):
        copy = pltpu.make_async_remote_copy(
            src_ref=src, dst_ref=dst, send_sem=send_sem, recv_sem=recv_sem,
            device_id=device, device_id_type=MESH,
        )
        copy.start()
        return copy

    stat_copies = [
        send(stat_mine, stat_peer.at[k - 1], stat_send.at[k - 1], stat_recv.at[k - 1], spot_peer_id(k))
        for k in range(1, spot_n)
    ]
    loads[chunks + 2].start()
    loads[chunks + 3].start()
    loads[chunks].wait()
    loads[chunks + 1].wait()
    expr_t[...] = expr[...].astype(jnp.float32).T.astype(jnp.bfloat16)
    flipped = target[...].T
    target_t[...] = flipped.reshape(target_t.shape)
    spot_target = jnp.sum(flipped * flipped, axis=0, keepdims=True)
    own_target = target_t[my_cell]
    gene_mine[2:3, :] = to_row(jnp.sum(own_target * own_target, axis=1, keepdims=True), mask)
    for copy in stat_copies:
        copy.wait()

    local_max = stat_mine[:chunks, :]
    row_max = local_max
    for k in range(spot_n - 1):
        row_max = jnp.maximum(row_max, stat_peer[k, :chunks, :])
    row_total = stat_mine[chunks:, :] * jnp.exp(local_max - row_max)
    for k in range(spot_n - 1):
        row_total = row_total + stat_peer[k, chunks:, :] * jnp.exp(stat_peer[k, :chunks, :] - row_max)
    factor = jnp.exp(local_max - row_max) / row_total
    for i in range(chunks):
        part_rows = slice(i * LANES, (i + 1) * LANES)
        prob = probs[part_rows, :] * to_column(factor[i : i + 1, :], mask)
        probs[part_rows, :] = prob
        weights[part_rows, :] = prob.astype(jnp.bfloat16)
    partial = jnp.dot(expr_t[...], weights[...], preferred_element_type=jnp.float32)
    part[...] = partial.astype(part.dtype).reshape(part.shape)
    own_part[...] = partial.reshape(own_part.shape)

    part_copies = [
        send(part.at[lax.rem(my_cell + k, cell_n)], part_peer.at[k - 1], part_send.at[k - 1],
             part_recv.at[k - 1], cell_peer(k))
        for k in range(1, cell_n)
    ]
    for copy in part_copies:
        copy.wait()
    predicted = own_part[my_cell]
    for k in range(cell_n - 1):
        predicted = predicted + part_peer[k].astype(jnp.float32)

    shared[my_cell] = predicted.astype(shared.dtype)
    shared_copies = [
        send(shared.at[my_cell], shared.at[my_cell], shared_send.at[k - 1], shared_recv.at[k - 1],
             cell_peer(k))
        for k in range(1, cell_n)
    ]
    gene_mine[0:1, :] = to_row(jnp.sum(predicted * own_target, axis=1, keepdims=True), mask)
    gene_mine[1:2, :] = to_row(jnp.sum(predicted * predicted, axis=1, keepdims=True), mask)
    gene_copies = [
        send(gene_mine, gene_peer.at[my_cell, k], gene_send.at[a, k], gene_recv.at[a, k], other(a, k))
        for a, k in others
    ]
    gene_peer[my_cell, 0] = gene_mine[...]
    for copy in shared_copies:
        copy.wait()
    predicted = shared[...].astype(jnp.float32).reshape(genes, width)
    wanted = target_t[...].reshape(genes, width)
    spot_dot = jnp.sum(predicted * wanted, axis=0, keepdims=True)
    spot_pred = jnp.sum(predicted * predicted, axis=0, keepdims=True)
    spot_scale = lax.rsqrt((spot_pred + norm_epsilon) * (spot_target + norm_epsilon))
    spot_lean = spot_dot / (spot_pred + norm_epsilon)
    by_spot = (wanted - spot_lean * predicted) * spot_scale
    for copy in gene_copies:
        copy.wait()
    for c in range(cell_n):
        span = slice(c * own_genes, (c + 1) * own_genes)
        gene_sums = gene_peer[c, 0]
        for k in range(1, spot_n):
            gene_sums = gene_sums + gene_peer[c, k]
        gene_scale = lax.rsqrt((gene_sums[1:2] + norm_epsilon) * (gene_sums[2:3] + norm_epsilon))
        gene_lean = gene_sums[0:1] / (gene_sums[1:2] + norm_epsilon)
        gene_scale = to_column(gene_scale, mask, own_genes)
        gene_lean = to_column(gene_lean, mask, own_genes)
        by_gene = (wanted[span] - gene_lean * predicted[span]) * gene_scale
        grads[span, :] = (-loss_weight * (by_spot[span] + ratio * by_gene)).astype(jnp.bfloat16)
    grad_all = grads[...]
    for i in range(chunks):
        part_rows = slice(i * LANES, (i + 1) * LANES)
        prob_grad = jnp.dot(expr[part_rows, :], grad_all, preferred_element_type=jnp.float32)
        prob_grads[part_rows, :] = prob_grad
        dots_mine[i : i + 1, :] = to_row(
            jnp.sum(probs[part_rows, :] * prob_grad, axis=1, keepdims=True), mask
        )
    dots_copies = [
        send(dots_mine, dots_peer.at[k - 1], dots_send.at[k - 1], dots_recv.at[k - 1], spot_peer_id(k))
        for k in range(1, spot_n)
    ]
    loads[chunks + 2].wait()
    loads[chunks + 3].wait()
    for copy in dots_copies:
        copy.wait()
    row_dot = dots_mine[...]
    for k in range(spot_n - 1):
        row_dot = row_dot + dots_peer[k]
    row_dots[...] = row_dot


def update_kernel(
    logits, first, second, probs, prob_grads, row_dots, new_logits, new_first, new_second
):
    at = pl.program_id(0)
    mask = eye_mask()
    per = new_logits.shape[0] // LANES
    for j in range(per):
        span = slice(j * LANES, (j + 1) * LANES)
        row = at * per + j
        rows = pl.ds(pl.multiple_of(row * LANES, LANES), LANES)
        row_dot = to_column(row_dots[pl.ds(row, 1), :], mask)
        logit_grad = probs[rows, :] * (prob_grads[rows, :] - row_dot)
        first_new = beta_one * first[rows, :].astype(jnp.float32) + (1.0 - beta_one) * logit_grad
        second_new = (
            beta_two * second[rows, :].astype(jnp.float32)
            + (1.0 - beta_two) * logit_grad * logit_grad
        )
        first_hat = first_new * (learn_rate / (1.0 - beta_one**adam_count))
        second_hat = second_new * (1.0 / (1.0 - beta_two**adam_count))
        new_logits[span, :] = logits[rows, :] - first_hat / (second_hat * lax.rsqrt(second_hat) + adam_epsilon)
        new_first[span, :] = first_new.astype(jnp.bfloat16)
        new_second[span, :] = second_new.astype(jnp.bfloat16)


def body(cell_n, spot_n, logits, first_moment, second_moment, cell_expr, spot_expr):
    rows, width = logits.shape
    genes = cell_expr.shape[1]
    own_genes = genes // cell_n
    chunks = rows // LANES
    f32 = jnp.float32
    dma = pltpu.SemaphoreType.DMA
    in_hbm = pl.BlockSpec(memory_space=pltpu.HBM)
    in_vmem = pl.BlockSpec(memory_space=pltpu.VMEM)
    cell_sem = dma((cell_n - 1,))
    spot_sem = dma((spot_n - 1,))
    all_sem = dma((cell_n, spot_n))
    like = [jax.ShapeDtypeStruct(x.shape, x.dtype) for x in (logits, first_moment, second_moment)]
    operands = (logits, cell_expr, spot_expr, first_moment, second_moment)
    held = pl.pallas_call(
        functools.partial(exchange_kernel, cell_n, spot_n, rows * cell_n, width * spot_n),
        out_shape=(*like, like[0], like[0], jax.ShapeDtypeStruct((chunks, LANES), f32)),
        in_specs=[in_hbm] * 5,
        out_specs=(in_vmem,) * 6,
        scratch_shapes=[
            pltpu.VMEM((rows, genes), jnp.bfloat16),
            pltpu.VMEM((width, genes), f32),
            pltpu.VMEM((rows, width), jnp.bfloat16),
            pltpu.VMEM((genes, rows), jnp.bfloat16),
            pltpu.VMEM((cell_n, own_genes, width), f32),
            pltpu.VMEM((cell_n, own_genes, width), f32),
            pltpu.VMEM((cell_n, own_genes, width), WIRE),
            pltpu.VMEM((2 * chunks, LANES), f32),
            pltpu.VMEM((spot_n - 1, 2 * chunks, LANES), f32),
            pltpu.VMEM((cell_n - 1, own_genes, width), WIRE),
            pltpu.VMEM((3, LANES), f32),
            pltpu.VMEM((cell_n, spot_n, 3, LANES), f32),
            pltpu.VMEM((cell_n, own_genes, width), WIRE),
            pltpu.VMEM((genes, width), jnp.bfloat16),
            pltpu.VMEM((chunks, LANES), f32),
            pltpu.VMEM((spot_n - 1, chunks, LANES), f32),
            dma((chunks + 4,)),
            spot_sem, spot_sem, cell_sem, cell_sem,
            all_sem, all_sem, cell_sem, cell_sem, spot_sem, spot_sem,
        ],
        compiler_params=pltpu.CompilerParams(
            collective_id=0, has_side_effects=True, vmem_limit_bytes=24 << 20
        ),
        cost_estimate=pl.CostEstimate(
            flops=4 * rows * width * genes, bytes_accessed=32 * rows * width, transcendentals=rows * width
        ),
        name="exchange",
    )(*(pltpu.with_memory_space_constraint(x, pltpu.HBM) for x in operands))
    tile = 2 * LANES if rows % (2 * LANES) == 0 else LANES
    by_row = pl.BlockSpec((tile, width), lambda i: (i, 0))
    return pl.pallas_call(
        update_kernel,
        grid=(rows // tile,),
        out_shape=like,
        in_specs=[in_vmem] * 6,
        out_specs=(by_row, by_row, by_row),
        compiler_params=pltpu.CompilerParams(vmem_limit_bytes=16 << 20),
        name="update",
    )(*held)


def solution(mesh):
    placed = (
        P("cell", "spot"),
        P("cell", "spot"),
        P("cell", "spot"),
        P("cell", None),
        P("spot", None),
    )
    return jax.shard_map(
        functools.partial(body, mesh.shape["cell"], mesh.shape["spot"]),
        mesh=mesh,
        in_specs=placed,
        out_specs=(P("cell", "spot"), P("cell", "spot"), P("cell", "spot")),
        check_vma=False,
    )
```

```python
import functools

import jax
import jax.numpy as jnp
from jax import lax
from jax.experimental import pallas as pl
from jax.experimental.pallas import tpu as pltpu
from jax.sharding import PartitionSpec as P

beta_one = 0.9
beta_two = 0.99
learn_rate = 0.1
adam_epsilon = 1e-08
norm_epsilon = 1e-06
adam_count = 10

MESH = pl.DeviceIdType.MESH
LANES = 128
WIRE = jnp.bfloat16


def eye_mask():
    row = lax.broadcasted_iota(jnp.int32, (LANES, LANES), 0)
    lane = lax.broadcasted_iota(jnp.int32, (LANES, LANES), 1)
    return row == lane


def to_row(column, mask):
    wide = jnp.broadcast_to(column, (column.shape[0], LANES))
    return jnp.sum(jnp.where(mask[: column.shape[0]], wide, 0.0), axis=0, keepdims=True)


def to_column(row, mask, count=LANES):
    wide = jnp.broadcast_to(row, (count, LANES))
    return jnp.sum(jnp.where(mask[:count], wide, 0.0), axis=1, keepdims=True)


def exchange_kernel(
    cell_n, spot_n, cells, spots,
    logits_hbm, expr_hbm, target_hbm, first_hbm, second_hbm,
    logits, first, second, probs, prob_grads, row_dots,
    first_in, second_in, expr, target, weights, expr_t, target_t, own_part, part,
    stat_mine, stat_peer, part_peer, gene_mine, gene_peer, shared, grads, dots_mine, dots_peer,
    load_sem, stat_send, stat_recv, part_send, part_recv,
    gene_send, gene_recv, shared_send, shared_recv, dots_send, dots_recv,
):
    rows, width = logits.shape
    genes = expr.shape[1]
    own_genes = genes // cell_n
    chunks = rows // LANES
    loss_weight = float(genes * cells) ** 0.5
    ratio = spots / genes
    my_cell = lax.axis_index("cell")
    my_spot = lax.axis_index("spot")

    def cell_peer(k):
        return (lax.rem(my_cell + k, cell_n), my_spot)

    def spot_peer_id(k):
        return (my_cell, lax.rem(my_spot + k, spot_n))

    loads = [
        pltpu.make_async_copy(
            logits_hbm.at[pl.ds(i * LANES, LANES)], logits.at[pl.ds(i * LANES, LANES)], load_sem.at[i]
        )
        for i in range(chunks)
    ]
    loads.append(pltpu.make_async_copy(expr_hbm, expr, load_sem.at[chunks]))
    loads.append(pltpu.make_async_copy(target_hbm, target, load_sem.at[chunks + 1]))
    loads.append(pltpu.make_async_copy(first_hbm, first_in, load_sem.at[chunks + 2]))
    loads.append(pltpu.make_async_copy(second_hbm, second_in, load_sem.at[chunks + 3]))
    for load in loads[: chunks + 2]:
        load.start()
    others = [(a, k) for k in range(spot_n) for a in range(cell_n) if a or k][::-1]

    def other(a, k):
        return (lax.rem(my_cell + a, cell_n), lax.rem(my_spot + k, spot_n))

    barrier = pltpu.get_barrier_semaphore()
    for a, k in others:
        pl.semaphore_signal(barrier, inc=1, device_id=other(a, k), device_id_type=MESH)

    mask = eye_mask()

    for i in range(chunks):
        loads[i].wait()
        block = logits[i * LANES : (i + 1) * LANES, :]
        top = jnp.max(block, axis=1, keepdims=True)
        expo = jnp.exp(block - top)
        probs[i * LANES : (i + 1) * LANES, :] = expo
        stat_mine[i : i + 1, :] = to_row(top, mask)
        stat_mine[chunks + i : chunks + i + 1, :] = to_row(
            jnp.sum(expo, axis=1, keepdims=True), mask
        )

    pl.semaphore_wait(barrier, len(others))

    def send(src, dst, send_sem, recv_sem, device):
        copy = pltpu.make_async_remote_copy(
            src_ref=src, dst_ref=dst, send_sem=send_sem, recv_sem=recv_sem,
            device_id=device, device_id_type=MESH,
        )
        copy.start()
        return copy

    stat_copies = [
        send(stat_mine, stat_peer.at[k - 1], stat_send.at[k - 1], stat_recv.at[k - 1], spot_peer_id(k))
        for k in range(1, spot_n)
    ]
    loads[chunks + 2].start()
    loads[chunks + 3].start()
    loads[chunks].wait()
    loads[chunks + 1].wait()
    expr_t[...] = expr[...].astype(jnp.float32).T.astype(jnp.bfloat16)
    flipped = target[...].T
    target_t[...] = flipped.reshape(target_t.shape)
    spot_target = jnp.sum(flipped * flipped, axis=0, keepdims=True)
    own_target = target_t[my_cell]
    gene_mine[2:3, :] = to_row(jnp.sum(own_target * own_target, axis=1, keepdims=True), mask)
    for copy in stat_copies:
        copy.wait()

    local_max = stat_mine[:chunks, :]
    row_max = local_max
    for k in range(spot_n - 1):
        row_max = jnp.maximum(row_max, stat_peer[k, :chunks, :])
    row_total = stat_mine[chunks:, :] * jnp.exp(local_max - row_max)
    for k in range(spot_n - 1):
        row_total = row_total + stat_peer[k, chunks:, :] * jnp.exp(stat_peer[k, :chunks, :] - row_max)
    factor = jnp.exp(local_max - row_max) / row_total
    for i in range(chunks):
        part_rows = slice(i * LANES, (i + 1) * LANES)
        prob = probs[part_rows, :] * to_column(factor[i : i + 1, :], mask)
        probs[part_rows, :] = prob
        weights[part_rows, :] = prob.astype(jnp.bfloat16)
    partial = jnp.dot(expr_t[...], weights[...], preferred_element_type=jnp.float32)
    part[...] = partial.astype(part.dtype).reshape(part.shape)
    own_part[...] = partial.reshape(own_part.shape)

    part_copies = [
        send(part.at[lax.rem(my_cell + k, cell_n)], part_peer.at[k - 1], part_send.at[k - 1],
             part_recv.at[k - 1], cell_peer(k))
        for k in range(1, cell_n)
    ]
    for copy in part_copies:
        copy.wait()
    predicted = own_part[my_cell]
    for k in range(cell_n - 1):
        predicted = predicted + part_peer[k].astype(jnp.float32)

    shared[my_cell] = predicted.astype(shared.dtype)
    gene_mine[0:1, :] = to_row(jnp.sum(predicted * own_target, axis=1, keepdims=True), mask)
    gene_mine[1:2, :] = to_row(jnp.sum(predicted * predicted, axis=1, keepdims=True), mask)
    gene_copies = [
        send(gene_mine, gene_peer.at[my_cell, k], gene_send.at[a, k], gene_recv.at[a, k], other(a, k))
        for a, k in others
    ]
    shared_copies = [
        send(shared.at[my_cell], shared.at[my_cell], shared_send.at[k - 1], shared_recv.at[k - 1],
             cell_peer(k))
        for k in range(1, cell_n)
    ]
    gene_peer[my_cell, 0] = gene_mine[...]
    for copy in shared_copies:
        copy.wait()
    predicted = shared[...].astype(jnp.float32).reshape(genes, width)
    wanted = target_t[...].reshape(genes, width)
    spot_dot = jnp.sum(predicted * wanted, axis=0, keepdims=True)
    spot_pred = jnp.sum(predicted * predicted, axis=0, keepdims=True)
    spot_scale = lax.rsqrt((spot_pred + norm_epsilon) * (spot_target + norm_epsilon))
    spot_lean = spot_dot / (spot_pred + norm_epsilon)
    by_spot = (wanted - spot_lean * predicted) * spot_scale
    for copy in gene_copies:
        copy.wait()
    for c in range(cell_n):
        span = slice(c * own_genes, (c + 1) * own_genes)
        gene_sums = gene_peer[c, 0]
        for k in range(1, spot_n):
            gene_sums = gene_sums + gene_peer[c, k]
        gene_scale = lax.rsqrt((gene_sums[1:2] + norm_epsilon) * (gene_sums[2:3] + norm_epsilon))
        gene_lean = gene_sums[0:1] / (gene_sums[1:2] + norm_epsilon)
        gene_scale = to_column(gene_scale, mask, own_genes)
        gene_lean = to_column(gene_lean, mask, own_genes)
        by_gene = (wanted[span] - gene_lean * predicted[span]) * gene_scale
        grads[span, :] = (-loss_weight * (by_spot[span] + ratio * by_gene)).astype(jnp.bfloat16)
    grad_all = grads[...]
    for i in range(chunks):
        part_rows = slice(i * LANES, (i + 1) * LANES)
        prob_grad = jnp.dot(expr[part_rows, :], grad_all, preferred_element_type=jnp.float32)
        prob_grads[part_rows, :] = prob_grad
        dots_mine[i : i + 1, :] = to_row(
            jnp.sum(probs[part_rows, :] * prob_grad, axis=1, keepdims=True), mask
        )
    dots_copies = [
        send(dots_mine, dots_peer.at[k - 1], dots_send.at[k - 1], dots_recv.at[k - 1], spot_peer_id(k))
        for k in range(1, spot_n)
    ]
    loads[chunks + 2].wait()
    loads[chunks + 3].wait()
    for i in range(chunks):
        part_rows = slice(i * LANES, (i + 1) * LANES)
        first[part_rows, :] = beta_one * first_in[part_rows, :].astype(jnp.float32)
        second[part_rows, :] = beta_two * second_in[part_rows, :].astype(jnp.float32)
    for copy in dots_copies:
        copy.wait()
    row_dot = dots_mine[...]
    for k in range(spot_n - 1):
        row_dot = row_dot + dots_peer[k]
    row_dots[...] = row_dot


def update_kernel(
    logits, first, second, probs, prob_grads, row_dots,
    logits_hbm, first_hbm, second_hbm,
    new_logits, new_first, new_second, store_sem,
):
    mask = eye_mask()
    stores = []
    for i in range(row_dots.shape[0]):
        span = pl.ds(i * LANES, LANES)
        row_dot = to_column(row_dots[i : i + 1, :], mask)
        logit_grad = probs[span, :] * (prob_grads[span, :] - row_dot)
        first_new = first[span, :] + (1.0 - beta_one) * logit_grad
        second_new = second[span, :] + (1.0 - beta_two) * logit_grad * logit_grad
        first_hat = first_new * (learn_rate / (1.0 - beta_one**adam_count))
        second_hat = second_new * (1.0 / (1.0 - beta_two**adam_count))
        new_logits[span, :] = logits[span, :] - first_hat / (
            second_hat * lax.rsqrt(second_hat) + adam_epsilon
        )
        new_first[span, :] = first_new.astype(jnp.bfloat16)
        new_second[span, :] = second_new.astype(jnp.bfloat16)
        pairs = ((new_logits, logits_hbm), (new_first, first_hbm), (new_second, second_hbm))
        for j, (held, out) in enumerate(pairs):
            copy = pltpu.make_async_copy(held.at[span], out.at[span], store_sem.at[i, j])
            copy.start()
            stores.append(copy)
    for copy in stores:
        copy.wait()


def body(cell_n, spot_n, logits, first_moment, second_moment, cell_expr, spot_expr):
    rows, width = logits.shape
    genes = cell_expr.shape[1]
    own_genes = genes // cell_n
    chunks = rows // LANES
    f32 = jnp.float32
    dma = pltpu.SemaphoreType.DMA
    in_hbm = pl.BlockSpec(memory_space=pltpu.HBM)
    in_vmem = pl.BlockSpec(memory_space=pltpu.VMEM)
    cell_sem = dma((cell_n - 1,))
    spot_sem = dma((spot_n - 1,))
    all_sem = dma((cell_n, spot_n))
    like = [jax.ShapeDtypeStruct(x.shape, x.dtype) for x in (logits, first_moment, second_moment)]
    operands = (logits, cell_expr, spot_expr, first_moment, second_moment)
    held = pl.pallas_call(
        functools.partial(exchange_kernel, cell_n, spot_n, rows * cell_n, width * spot_n),
        out_shape=(*like[:1] * 5, jax.ShapeDtypeStruct((chunks, LANES), f32)),
        in_specs=[in_hbm] * 5,
        out_specs=(in_vmem,) * 6,
        scratch_shapes=[
            pltpu.VMEM((rows, width), jnp.bfloat16),
            pltpu.VMEM((rows, width), jnp.bfloat16),
            pltpu.VMEM((rows, genes), jnp.bfloat16),
            pltpu.VMEM((width, genes), f32),
            pltpu.VMEM((rows, width), jnp.bfloat16),
            pltpu.VMEM((genes, rows), jnp.bfloat16),
            pltpu.VMEM((cell_n, own_genes, width), f32),
            pltpu.VMEM((cell_n, own_genes, width), f32),
            pltpu.VMEM((cell_n, own_genes, width), WIRE),
            pltpu.VMEM((2 * chunks, LANES), f32),
            pltpu.VMEM((spot_n - 1, 2 * chunks, LANES), f32),
            pltpu.VMEM((cell_n - 1, own_genes, width), WIRE),
            pltpu.VMEM((3, LANES), f32),
            pltpu.VMEM((cell_n, spot_n, 3, LANES), f32),
            pltpu.VMEM((cell_n, own_genes, width), WIRE),
            pltpu.VMEM((genes, width), jnp.bfloat16),
            pltpu.VMEM((chunks, LANES), f32),
            pltpu.VMEM((spot_n - 1, chunks, LANES), f32),
            dma((chunks + 4,)),
            spot_sem, spot_sem, cell_sem, cell_sem,
            all_sem, all_sem, cell_sem, cell_sem, spot_sem, spot_sem,
        ],
        compiler_params=pltpu.CompilerParams(
            collective_id=0, has_side_effects=True, vmem_limit_bytes=24 << 20
        ),
        cost_estimate=pl.CostEstimate(
            flops=4 * rows * width * genes, bytes_accessed=32 * rows * width, transcendentals=rows * width
        ),
        name="exchange",
    )(*(pltpu.with_memory_space_constraint(x, pltpu.HBM) for x in operands))
    return pl.pallas_call(
        update_kernel,
        out_shape=like,
        in_specs=[in_vmem] * 6,
        out_specs=(in_hbm,) * 3,
        scratch_shapes=[pltpu.VMEM(x.shape, x.dtype) for x in like] + [dma((chunks, 3))],
        compiler_params=pltpu.CompilerParams(vmem_limit_bytes=16 << 20),
        name="update",
    )(*held)


def solution(mesh):
    placed = (
        P("cell", "spot"),
        P("cell", "spot"),
        P("cell", "spot"),
        P("cell", None),
        P("spot", None),
    )
    return jax.shard_map(
        functools.partial(body, mesh.shape["cell"], mesh.shape["spot"]),
        mesh=mesh,
        in_specs=placed,
        out_specs=(P("cell", "spot"), P("cell", "spot"), P("cell", "spot")),
        check_vma=False,
    )
```

```python
import functools

import jax
import jax.numpy as jnp
from jax import lax
from jax.experimental import pallas as pl
from jax.experimental.pallas import tpu as pltpu
from jax.sharding import PartitionSpec as P

beta_one = 0.9
beta_two = 0.99
learn_rate = 0.1
adam_epsilon = 1e-08
norm_epsilon = 1e-06
adam_count = 10

MESH = pl.DeviceIdType.MESH
LANES = 128
WIRE = jnp.bfloat16


def eye_mask():
    row = lax.broadcasted_iota(jnp.int32, (LANES, LANES), 0)
    lane = lax.broadcasted_iota(jnp.int32, (LANES, LANES), 1)
    return row == lane


def to_row(column, mask):
    wide = jnp.broadcast_to(column, (column.shape[0], LANES))
    return jnp.sum(jnp.where(mask[: column.shape[0]], wide, 0.0), axis=0, keepdims=True)


def to_column(row, mask, count=LANES):
    wide = jnp.broadcast_to(row, (count, LANES))
    return jnp.sum(jnp.where(mask[:count], wide, 0.0), axis=1, keepdims=True)


def exchange_kernel(
    cell_n, spot_n, cells, spots,
    logits_hbm, expr_hbm, target_hbm, first_hbm, second_hbm,
    logits, first, second, probs, prob_grads, row_dots,
    first_in, second_in, expr, target, weights, expr_t, target_t, own_part, part,
    stat_mine, stat_peer, part_peer, gene_mine, gene_peer, shared, grads, dots_mine, dots_peer,
    load_sem, stat_send, stat_recv, part_send, part_recv,
    gene_send, gene_recv, shared_send, shared_recv, dots_send, dots_recv,
):
    rows, width = logits.shape
    genes = expr.shape[1]
    own_genes = genes // cell_n
    chunks = rows // LANES
    loss_weight = float(genes * cells) ** 0.5
    ratio = spots / genes
    my_cell = lax.axis_index("cell")
    my_spot = lax.axis_index("spot")

    def cell_peer(k):
        return (lax.rem(my_cell + k, cell_n), my_spot)

    def spot_peer_id(k):
        return (my_cell, lax.rem(my_spot + k, spot_n))

    loads = [
        pltpu.make_async_copy(
            logits_hbm.at[pl.ds(i * LANES, LANES)], logits.at[pl.ds(i * LANES, LANES)], load_sem.at[i]
        )
        for i in range(chunks)
    ]
    loads.append(pltpu.make_async_copy(expr_hbm, expr, load_sem.at[chunks]))
    loads.append(pltpu.make_async_copy(target_hbm, target, load_sem.at[chunks + 1]))
    loads.append(pltpu.make_async_copy(first_hbm, first_in, load_sem.at[chunks + 2]))
    loads.append(pltpu.make_async_copy(second_hbm, second_in, load_sem.at[chunks + 3]))
    for load in loads[: chunks + 2]:
        load.start()
    others = [(a, k) for k in range(spot_n) for a in range(cell_n) if a or k][::-1]

    def other(a, k):
        return (lax.rem(my_cell + a, cell_n), lax.rem(my_spot + k, spot_n))

    barrier = pltpu.get_barrier_semaphore()
    for a, k in others:
        pl.semaphore_signal(barrier, inc=1, device_id=other(a, k), device_id_type=MESH)

    mask = eye_mask()

    for i in range(chunks):
        loads[i].wait()
        block = logits[i * LANES : (i + 1) * LANES, :]
        top = jnp.max(block, axis=1, keepdims=True)
        expo = jnp.exp(block - top)
        probs[i * LANES : (i + 1) * LANES, :] = expo
        stat_mine[i : i + 1, :] = to_row(top, mask)
        stat_mine[chunks + i : chunks + i + 1, :] = to_row(
            jnp.sum(expo, axis=1, keepdims=True), mask
        )

    pl.semaphore_wait(barrier, len(others))

    def send(src, dst, send_sem, recv_sem, device):
        copy = pltpu.make_async_remote_copy(
            src_ref=src, dst_ref=dst, send_sem=send_sem, recv_sem=recv_sem,
            device_id=device, device_id_type=MESH,
        )
        copy.start()
        return copy

    stat_copies = [
        send(stat_mine, stat_peer.at[k - 1], stat_send.at[k - 1], stat_recv.at[k - 1], spot_peer_id(k))
        for k in range(spot_n - 1, 0, -1)
    ]
    loads[chunks + 2].start()
    loads[chunks + 3].start()
    loads[chunks].wait()
    loads[chunks + 1].wait()
    expr_t[...] = expr[...].astype(jnp.float32).T.astype(jnp.bfloat16)
    flipped = target[...].T
    target_t[...] = flipped.reshape(target_t.shape)
    spot_target = jnp.sum(flipped * flipped, axis=0, keepdims=True)
    own_target = target_t[my_cell]
    gene_mine[2:3, :] = to_row(jnp.sum(own_target * own_target, axis=1, keepdims=True), mask)
    for copy in stat_copies:
        copy.wait()

    local_max = stat_mine[:chunks, :]
    row_max = local_max
    for k in range(spot_n - 1):
        row_max = jnp.maximum(row_max, stat_peer[k, :chunks, :])
    row_total = stat_mine[chunks:, :] * jnp.exp(local_max - row_max)
    for k in range(spot_n - 1):
        row_total = row_total + stat_peer[k, chunks:, :] * jnp.exp(stat_peer[k, :chunks, :] - row_max)
    factor = jnp.exp(local_max - row_max) / row_total
    for i in range(chunks):
        part_rows = slice(i * LANES, (i + 1) * LANES)
        prob = probs[part_rows, :] * to_column(factor[i : i + 1, :], mask)
        probs[part_rows, :] = prob
        weights[part_rows, :] = prob.astype(jnp.bfloat16)
    partial = jnp.dot(expr_t[...], weights[...], preferred_element_type=jnp.float32)
    part[...] = partial.astype(part.dtype).reshape(part.shape)
    own_part[...] = partial.reshape(own_part.shape)

    part_copies = [
        send(part.at[lax.rem(my_cell + k, cell_n)], part_peer.at[k - 1], part_send.at[k - 1],
             part_recv.at[k - 1], cell_peer(k))
        for k in range(1, cell_n)
    ]
    for copy in part_copies:
        copy.wait()
    predicted = own_part[my_cell]
    for k in range(cell_n - 1):
        predicted = predicted + part_peer[k].astype(jnp.float32)

    shared[my_cell] = predicted.astype(shared.dtype)
    gene_mine[0:1, :] = to_row(jnp.sum(predicted * own_target, axis=1, keepdims=True), mask)
    gene_mine[1:2, :] = to_row(jnp.sum(predicted * predicted, axis=1, keepdims=True), mask)
    gene_copies = [
        send(gene_mine, gene_peer.at[my_cell, k], gene_send.at[a, k], gene_recv.at[a, k], other(a, k))
        for a, k in others
    ]
    shared_copies = [
        send(shared.at[my_cell], shared.at[my_cell], shared_send.at[k - 1], shared_recv.at[k - 1],
             cell_peer(k))
        for k in range(1, cell_n)
    ]
    gene_peer[my_cell, 0] = gene_mine[...]
    for copy in shared_copies:
        copy.wait()
    predicted = shared[...].astype(jnp.float32).reshape(genes, width)
    wanted = target_t[...].reshape(genes, width)
    spot_dot = jnp.sum(predicted * wanted, axis=0, keepdims=True)
    spot_pred = jnp.sum(predicted * predicted, axis=0, keepdims=True)
    spot_scale = lax.rsqrt((spot_pred + norm_epsilon) * (spot_target + norm_epsilon))
    spot_lean = spot_dot / (spot_pred + norm_epsilon)
    by_spot = (wanted - spot_lean * predicted) * spot_scale
    for copy in gene_copies:
        copy.wait()
    for c in range(cell_n):
        span = slice(c * own_genes, (c + 1) * own_genes)
        gene_sums = gene_peer[c, 0]
        for k in range(1, spot_n):
            gene_sums = gene_sums + gene_peer[c, k]
        gene_scale = lax.rsqrt((gene_sums[1:2] + norm_epsilon) * (gene_sums[2:3] + norm_epsilon))
        gene_lean = gene_sums[0:1] / (gene_sums[1:2] + norm_epsilon)
        gene_scale = to_column(gene_scale, mask, own_genes)
        gene_lean = to_column(gene_lean, mask, own_genes)
        by_gene = (wanted[span] - gene_lean * predicted[span]) * gene_scale
        grads[span, :] = (-loss_weight * (by_spot[span] + ratio * by_gene)).astype(jnp.bfloat16)
    grad_all = grads[...]
    for i in range(chunks):
        part_rows = slice(i * LANES, (i + 1) * LANES)
        prob_grad = jnp.dot(expr[part_rows, :], grad_all, preferred_element_type=jnp.float32)
        prob_grads[part_rows, :] = prob_grad
        dots_mine[i : i + 1, :] = to_row(
            jnp.sum(probs[part_rows, :] * prob_grad, axis=1, keepdims=True), mask
        )
    dots_copies = [
        send(dots_mine, dots_peer.at[k - 1], dots_send.at[k - 1], dots_recv.at[k - 1], spot_peer_id(k))
        for k in range(spot_n - 1, 0, -1)
    ]
    loads[chunks + 2].wait()
    loads[chunks + 3].wait()
    for i in range(chunks):
        part_rows = slice(i * LANES, (i + 1) * LANES)
        first[part_rows, :] = beta_one * first_in[part_rows, :].astype(jnp.float32)
        second[part_rows, :] = beta_two * second_in[part_rows, :].astype(jnp.float32)
    for copy in dots_copies:
        copy.wait()
    row_dot = dots_mine[...]
    for k in range(spot_n - 1):
        row_dot = row_dot + dots_peer[k]
    row_dots[...] = row_dot


def update_kernel(
    logits, first, second, probs, prob_grads, row_dots,
    logits_hbm, first_hbm, second_hbm,
    new_logits, new_first, new_second, store_sem,
):
    mask = eye_mask()
    stores = []
    for i in range(row_dots.shape[0]):
        span = pl.ds(i * LANES, LANES)
        row_dot = to_column(row_dots[i : i + 1, :], mask)
        logit_grad = probs[span, :] * (prob_grads[span, :] - row_dot)
        first_new = first[span, :] + (1.0 - beta_one) * logit_grad
        second_new = second[span, :] + (1.0 - beta_two) * logit_grad * logit_grad
        first_hat = first_new * (learn_rate / (1.0 - beta_one**adam_count))
        second_hat = second_new * (1.0 / (1.0 - beta_two**adam_count))
        new_logits[span, :] = logits[span, :] - first_hat / (
            second_hat * lax.rsqrt(second_hat) + adam_epsilon
        )
        new_first[span, :] = first_new.astype(jnp.bfloat16)
        new_second[span, :] = second_new.astype(jnp.bfloat16)
        pairs = ((new_logits, logits_hbm), (new_first, first_hbm), (new_second, second_hbm))
        for j, (held, out) in enumerate(pairs):
            copy = pltpu.make_async_copy(held.at[span], out.at[span], store_sem.at[i, j])
            copy.start()
            stores.append(copy)
    for copy in stores:
        copy.wait()


def body(cell_n, spot_n, logits, first_moment, second_moment, cell_expr, spot_expr):
    rows, width = logits.shape
    genes = cell_expr.shape[1]
    own_genes = genes // cell_n
    chunks = rows // LANES
    f32 = jnp.float32
    dma = pltpu.SemaphoreType.DMA
    in_hbm = pl.BlockSpec(memory_space=pltpu.HBM)
    in_vmem = pl.BlockSpec(memory_space=pltpu.VMEM)
    cell_sem = dma((cell_n - 1,))
    spot_sem = dma((spot_n - 1,))
    all_sem = dma((cell_n, spot_n))
    like = [jax.ShapeDtypeStruct(x.shape, x.dtype) for x in (logits, first_moment, second_moment)]
    operands = (logits, cell_expr, spot_expr, first_moment, second_moment)
    held = pl.pallas_call(
        functools.partial(exchange_kernel, cell_n, spot_n, rows * cell_n, width * spot_n),
        out_shape=(*like[:1] * 5, jax.ShapeDtypeStruct((chunks, LANES), f32)),
        in_specs=[in_hbm] * 5,
        out_specs=(in_vmem,) * 6,
        scratch_shapes=[
            pltpu.VMEM((rows, width), jnp.bfloat16),
            pltpu.VMEM((rows, width), jnp.bfloat16),
            pltpu.VMEM((rows, genes), jnp.bfloat16),
            pltpu.VMEM((width, genes), f32),
            pltpu.VMEM((rows, width), jnp.bfloat16),
            pltpu.VMEM((genes, rows), jnp.bfloat16),
            pltpu.VMEM((cell_n, own_genes, width), f32),
            pltpu.VMEM((cell_n, own_genes, width), f32),
            pltpu.VMEM((cell_n, own_genes, width), WIRE),
            pltpu.VMEM((2 * chunks, LANES), f32),
            pltpu.VMEM((spot_n - 1, 2 * chunks, LANES), f32),
            pltpu.VMEM((cell_n - 1, own_genes, width), WIRE),
            pltpu.VMEM((3, LANES), f32),
            pltpu.VMEM((cell_n, spot_n, 3, LANES), f32),
            pltpu.VMEM((cell_n, own_genes, width), WIRE),
            pltpu.VMEM((genes, width), jnp.bfloat16),
            pltpu.VMEM((chunks, LANES), f32),
            pltpu.VMEM((spot_n - 1, chunks, LANES), f32),
            dma((chunks + 4,)),
            spot_sem, spot_sem, cell_sem, cell_sem,
            all_sem, all_sem, cell_sem, cell_sem, spot_sem, spot_sem,
        ],
        compiler_params=pltpu.CompilerParams(
            collective_id=0, has_side_effects=True, vmem_limit_bytes=24 << 20
        ),
        cost_estimate=pl.CostEstimate(
            flops=4 * rows * width * genes, bytes_accessed=32 * rows * width, transcendentals=rows * width
        ),
        name="exchange",
    )(*(pltpu.with_memory_space_constraint(x, pltpu.HBM) for x in operands))
    return pl.pallas_call(
        update_kernel,
        out_shape=like,
        in_specs=[in_vmem] * 6,
        out_specs=(in_hbm,) * 3,
        scratch_shapes=[pltpu.VMEM(x.shape, x.dtype) for x in like] + [dma((chunks, 3))],
        compiler_params=pltpu.CompilerParams(vmem_limit_bytes=16 << 20),
        name="update",
    )(*held)


def solution(mesh):
    placed = (
        P("cell", "spot"),
        P("cell", "spot"),
        P("cell", "spot"),
        P("cell", None),
        P("spot", None),
    )
    return jax.shard_map(
        functools.partial(body, mesh.shape["cell"], mesh.shape["spot"]),
        mesh=mesh,
        in_specs=placed,
        out_specs=(P("cell", "spot"), P("cell", "spot"), P("cell", "spot")),
        check_vma=False,
    )
```
